32 devices in a mesh: groups: 2 (over x), tensor: 16 (over z, y, core).
Axes of the slice: x: 2, y: 2, z: 4, core: 2. Of those that a mesh axis runs over, the one named last changes fastest.
Arguments:
- image_features: bfloat16 [256, 12800], P('groups', 'tensor'), parts along dimension 0, may hold values from -6 to 6
- image_counts: int32 [4], P('groups'), parts along dimension 0, may hold values from 1 to 64, 80 in all
- slot_position: int32 [256], P('groups'), parts along dimension 0, may hold values from 0 to 255, as said below
- text_ids: int32 [512], P('groups'), parts along dimension 0, may hold values from 0 to 49151
- norm_gain: float32 [12800], replicated, may hold values from 0.5 to 1.5
- norm_bias: float32 [12800], replicated, may hold values from -3 to 3
- proj_first: bfloat16 [6144, 12800], P('tensor'), may hold values from -0.0546875 to 0.0546875
- proj_second: bfloat16 [6144, 6144], P('tensor'), may hold values from -0.078125 to 0.078125
- embedding: bfloat16 [6144, 49152], P('tensor'), may hold values from -6 to 6
- rms_gain: float32 [6144], replicated, may hold values from 0.5 to 1.5
- gate_weight: bfloat16 [6144, 16384], P(None, 'tensor'), may hold values from -0.109375 to 0.109375
- up_weight: bfloat16 [6144, 16384], P(None, 'tensor'), may hold values from -0.109375 to 0.109375
- down_weight: bfloat16 [16384, 6144], P('tensor'), may hold values from -0.046875 to 0.046875
- output_grad: bfloat16 [512, 6144], P('groups', 'tensor'), parts along dimension 0, may hold values from -6 to 6
Outputs:
- input_grad: float32 [512, 6144], P('groups', 'tensor'), parts along dimension 0
- second_grad: float32 [12288, 6144], P(('groups', 'tensor')), parts along dimension 0
The draws below stay inside these ranges and needn't reach their ends.
There are 2 independent parts, one for each index of `groups`. The reference program is written for one: setup_inputs(seed, part) draws one part's arguments, and reference() takes and returns one part's arrays. A program takes and returns all parts, laid end to end along the dimension named above; an argument that names none is the same for every part. Nothing has to cross between parts.
Inputs may be any that keep to these rules, and one draw needn't show every extreme that they name: `image_counts`: the counts sum to 80. `slot_position`: the 128 positions are distinct.
All inputs are finite; a program needn't handle non-finite values.
Results may differ from the reference program's by a relative error of at most 0.0079.
Values may be sent and summed in bfloat16 or wider, within the bound.
No kernel may reach another device: no remote copies, remote signals or barrier semaphores. Data moves between devices by JAX's collectives and lax.ppermute only.
A program may use at most 192 MiB of HBM per device.

```python
import math
import jax
import jax.numpy as jnp
import numpy as np
from jax import lax

PIX = 12800
D = 6144
FF = 16384
VOCAB = 49152
CAP = 64
IMAGES = 2
SLOTS = 128
LIVE = 80
SEQ = 256


def draw_slot_position(key, part):
    return jax.random.permutation(jax.random.fold_in(key, 17), SEQ)[:SLOTS].astype(jnp.int32)


def place_ends(array, rng, least, top_value):
    dims = array.shape
    index_at = [jax.random.randint(jax.random.fold_in(rng, axis), (), 0, dims[axis]) for axis in range(len(dims))]
    array = array.at[tuple(index_at)].set(least)
    longest = dims.index(max(dims))
    index_at[longest] = (index_at[longest] + 1) % dims[longest]
    return array.at[tuple(index_at)].set(top_value)


def raised(values, key, source, target, shards_of, factor):
    def block_of(axis_at):
        return (jnp.arange(values.shape[axis_at]) // (values.shape[axis_at] // shards_of)).reshape((-1,) + (1,) * (values.ndim - 1 - axis_at))

    one_side = jax.random.permutation(key, shards_of)[block_of(target)]
    other_side = (block_of(target) + shards_of // 2) % shards_of
    return jnp.where((block_of(source) == one_side) | (block_of(source) == other_side), factor * values, values)


def block_levels(stream_key, shape, cuts, low, largest):
    def one(dim, shards_of):
        draws = jax.random.uniform(jax.random.fold_in(jax.random.fold_in(stream_key, 6), dim), (shards_of,), jnp.float32, low / len(cuts), largest / len(cuts))
        return jnp.repeat(jnp.exp(draws), shape[dim] // shards_of).reshape((-1,) + (1,) * (len(shape) - dim - 1))

    level = one(*cuts[0])
    for cut in cuts[1:]:
        level = level * one(*cut)
    return level


def cumulative_ranks(amount, lean):
    weights = [(1 << 20) // math.isqrt(rank ** lean) + 1 for rank in range(1, amount + 1)]
    scale = 1 + sum(weights) // (1 << 30)
    return np.cumsum(np.array([max(1, weight // scale) for weight in weights]))


def ranked(rng, dims, count, skew):
    table = cumulative_ranks(count, skew)
    lot = jax.random.randint(jax.random.fold_in(rng, 1), dims, 0, int(table[count - 1]))
    rank = jnp.searchsorted(jnp.asarray(table, jnp.int32), lot, side="right")
    return jax.random.permutation(jax.random.fold_in(rng, 2), count)[rank].astype(jnp.int32)


def split_up(number_of, total, most, slope):
    loads = [(1 << 20) // math.isqrt(standing ** slope) + 1 for standing in range(2, number_of + 1)]
    surplus, given = total - most - (number_of - 1), [1] * (number_of - 1)
    while surplus > 0:
        free = [i for i in range(number_of - 1) if given[i] < most]
        whole, left = sum([loads[i] for i in free]), surplus
        for i in free:
            extra = min(most - given[i], max(1, left * loads[i] // whole), surplus)
            given[i] = given[i] + extra
            surplus = surplus - extra
    return np.array([most] + given)


def uneven(stream_key, count, total, limit, lean):
    if count == 2:
        one = jax.random.randint(stream_key, (), max(1, total - limit), min(limit, total - 1) + 1)
        return jnp.stack([one, total - one])
    tallies = jnp.asarray(split_up(count, total, limit, lean), jnp.int32)
    couples = (count - 1) // 2
    giver, sink = tallies[1:1 + 2 * couples:2], tallies[2:2 + 2 * couples:2]
    slack = jnp.minimum(giver - 1, limit - sink)
    passed = jax.random.randint(jax.random.fold_in(stream_key, 1), (couples,), 0, 1 << 20) % (slack + 1)
    tallies = tallies.at[1:1 + 2 * couples:2].set(giver - passed).at[2:2 + 2 * couples:2].set(sink + passed)
    return tallies[jax.random.permutation(jax.random.fold_in(stream_key, 2), count)]


def centred(rng, extent, scale, bound, shards=(), kind=jnp.bfloat16):
    loudness = block_levels(rng, extent, shards, -0.22, 0.18) if shards else 1.0
    entries = jax.random.normal(rng, extent, jnp.float32) * scale * loudness
    return jnp.minimum(jnp.maximum(entries, -bound), bound).astype(kind)


def bell_draw_with(rng, shape, deviation, reach, split, heavy, kind=jnp.bfloat16):
    result = deviation * jax.random.normal(rng, shape, jnp.float32)
    if split:
        result = result * block_levels(rng, shape, split, -0.22, 0.18)
    return jnp.clip(raised(result, jax.random.fold_in(rng, 3), *heavy), -reach, reach).astype(kind)


def setup_inputs(seed: int = 0, part: int = 0) -> dict:
    streams_of = jax.random.split(jax.random.key(seed), 15)
    part_keys = jax.random.split(jax.random.fold_in(streams_of[14], part), 15)
    return {
        "image_features": centred(part_keys[0], (SLOTS, PIX), 1.0, 6.0, ((1, 16),)),
        "image_counts": uneven(part_keys[1], IMAGES, LIVE, CAP, 2).astype(jnp.int32),
        "slot_position": draw_slot_position(jax.random.fold_in(jax.random.fold_in(streams_of[14], part), 71), part),
        "text_ids": place_ends(ranked(part_keys[3], (SEQ,), VOCAB, 2), jax.random.fold_in(part_keys[3], 3), 0, VOCAB - 1).astype(jnp.int32),
        "norm_gain": jnp.clip(1.0 + 0.1 * jax.random.normal(streams_of[4], (PIX,), jnp.float32), 0.5, 1.5),
        "norm_bias": centred(streams_of[5], (PIX,), 0.5, 3.0, (), jnp.float32),
        "proj_first": centred(streams_of[6], (D, PIX), PIX ** -0.5, 0.0546875, ((0, 16),)),
        "proj_second": centred(streams_of[7], (D, D), D ** -0.5, 0.078125, ((0, 16),)),
        "embedding": centred(streams_of[8], (D, VOCAB), 1.0, 6.0, ((0, 16),)),
        "rms_gain": jnp.clip(1.0 + 0.1 * jax.random.normal(streams_of[9], (D,), jnp.float32), 0.5, 1.5),
        "gate_weight": bell_draw_with(streams_of[10], (D, FF), D ** -0.5, 0.109375, ((1, 16),), (1, 0, 16, 2.0)),
        "up_weight": bell_draw_with(streams_of[11], (D, FF), D ** -0.5, 0.109375, ((1, 16),), (1, 0, 16, 2.0)),
        "down_weight": centred(streams_of[12], (FF, D), FF ** -0.5, 0.046875, ((0, 16),)),
        "output_grad": centred(part_keys[13], (SEQ, D), 1.0, 6.0, ((1, 16),)),
    }


def reference(image_features, image_counts, slot_position, text_ids, norm_gain, norm_bias, proj_first, proj_second, embedding, rms_gain, gate_weight, up_weight, down_weight, output_grad):
    slot_ids = jnp.arange(SLOTS, dtype=jnp.int32)
    is_live = slot_ids % CAP < jnp.repeat(image_counts, CAP, total_repeat_length=SLOTS)
    values = image_features.astype(jnp.float32)
    centre = values - lax.optimization_barrier(jnp.mean(values, axis=-1, keepdims=True))
    spread = lax.optimization_barrier(jnp.mean(centre * centre, axis=-1, keepdims=True))
    normed = (centre * lax.rsqrt(spread + 1e-05) * norm_gain + norm_bias).astype(jnp.bfloat16)
    hidden_pre = lax.dot_general(normed, proj_first, (((1,), (1,)), ((), ())), preferred_element_type=jnp.float32)
    hidden_act = jax.nn.gelu(hidden_pre, approximate=False).astype(jnp.bfloat16)
    projected = lax.dot_general(hidden_act, proj_second, (((1,), (1,)), ((), ())), preferred_element_type=jnp.float32).astype(jnp.bfloat16)
    target = jnp.where(is_live, slot_position, SEQ).astype(jnp.int32)
    text_rows = jnp.take(embedding, text_ids, axis=1).T
    tokens = text_rows.at[target].set(projected, mode='drop')
    token_values = tokens.astype(jnp.float32)
    inverse = lax.rsqrt(lax.optimization_barrier(jnp.mean(token_values * token_values, axis=-1, keepdims=True)) + 1e-05)
    unit = token_values * inverse
    normed_tokens = (unit * rms_gain).astype(jnp.bfloat16)
    gate_out = jnp.dot(normed_tokens, gate_weight, preferred_element_type=jnp.float32)
    up_out = jnp.dot(normed_tokens, up_weight, preferred_element_type=jnp.float32)
    hidden_grad = lax.dot_general(output_grad, down_weight, (((1,), (1,)), ((), ())), preferred_element_type=jnp.float32)
    sig_gate = jax.nn.sigmoid(gate_out)
    gate_grad = (hidden_grad * up_out * sig_gate * (1.0 + gate_out * (1.0 - sig_gate))).astype(jnp.bfloat16)
    up_grad = (hidden_grad * gate_out * sig_gate).astype(jnp.bfloat16)
    norm_grad = lax.dot_general(gate_grad, gate_weight, (((1,), (1,)), ((), ())), preferred_element_type=jnp.float32)
    norm_grad = norm_grad + lax.dot_general(up_grad, up_weight, (((1,), (1,)), ((), ())), preferred_element_type=jnp.float32)
    scaled = rms_gain * norm_grad
    row_dots = lax.optimization_barrier(jnp.sum(scaled * unit, axis=-1, keepdims=True))
    input_grad = output_grad.astype(jnp.float32) + inverse * (scaled - unit * row_dots / D)
    proj_grad = jnp.where(is_live[:, None], input_grad[slot_position], 0.0).astype(jnp.bfloat16)
    second_grad = lax.dot_general(proj_grad, hidden_act, (((0,), (0,)), ((), ())), preferred_element_type=jnp.float32)
    return (input_grad, second_grad)
```

```python
import functools

import jax
import jax.numpy as jnp
from jax import lax
from jax.experimental import pallas as pl
from jax.experimental.pallas import tpu as pltpu
from jax.sharding import PartitionSpec as P

LIVE = 80
AX = "tensor"
F32 = jnp.float32
BF16 = jnp.bfloat16
ANY = pl.BlockSpec(memory_space=pl.ANY)
SMEM = pl.BlockSpec(memory_space=pltpu.SMEM)
VMEM = pl.BlockSpec(memory_space=pltpu.VMEM)


def layer_norm(rows_in, gain_in, bias_in):
    values = rows_in.astype(jnp.float32)
    centre = values - jnp.mean(values, axis=-1, keepdims=True)
    spread = jnp.mean(centre * centre, axis=-1, keepdims=True)
    return (centre * lax.rsqrt(spread + 1e-05) * gain_in + bias_in).astype(jnp.bfloat16)


def send(x, partner, n):
    return lax.ppermute(x, AX, [(t, partner(t)) for t in range(n)])


def flip(x, mask, n):
    return send(x, lambda t: t ^ mask, n)


def down(x, d, n):
    return send(x, lambda t: (t - 4 * d) % n, n)


def up(x, d, n):
    return send(x, lambda t: (t + 4 * d) % n, n)


def device_of(t, q, n):
    depth = n // 4
    core, row, d = q // (2 * depth), q // depth % 2, q % depth
    return lax.rem(t // 4 + d, depth) * 4 + (t // 2 % 2 + row) % 2 * 2 + (t % 2 + core) % 2


def gather_blocks(x, n):
    own = [x] + [down(x, d, n) for d in range(1, n // 4)]
    other = [flip(p, 2, n) for p in own]
    four = own + other
    return four + [flip(p, 1, n) for p in four]


def gather_stacks(x, n):
    own = jnp.stack([x] + [down(x, d, n) for d in range(1, n // 4)])
    other = flip(own, 2, n)
    return [own, other, flip(own, 1, n), flip(other, 1, n)]


def scatter_sum(parts, n):
    near, far, near_pair, far_pair = parts
    depth = n // 4
    from_far = flip(far_pair, 1, n)
    from_near = flip(near_pair, 1, n)
    far_sum = (far.astype(F32) + from_far.astype(F32)).astype(BF16)
    from_row = flip(far_sum, 2, n)
    total = [
        near[d].astype(F32) + from_near[d].astype(F32) + from_row[d].astype(F32)
        for d in range(depth)
    ]
    arrived = [up(total[d].astype(BF16), d, n) for d in range(1, depth)]
    return functools.reduce(lambda a, b: a + b.astype(F32), arrived, total[0])


def flat_index(t):
    return jnp.reshape(t, (1,)).astype(jnp.int32)


def piece(refs, q):
    if len(refs[0].shape) == 2:
        return refs[q]
    per = refs[0].shape[0]
    return refs[q // per].at[q % per]


def columns_kernel(n, count, t_ref, *refs):
    ins, out, sems = refs[:count], refs[count], refs[count + 1]
    t = t_ref[0]
    cols = ins[0].shape[-1]
    copies = []
    for q in range(n):
        at = pl.multiple_of(device_of(t, q, n) * cols, 128)
        copies.append(
            pltpu.make_async_copy(piece(ins, q), out.at[:, pl.ds(at, cols)], sems.at[q])
        )
    for copy in copies:
        copy.start()
    for copy in copies:
        copy.wait()


def join_columns(pieces, t, n):
    rows, cols = pieces[0].shape[-2:]
    return pl.pallas_call(
        functools.partial(columns_kernel, n, len(pieces)),
        out_shape=jax.ShapeDtypeStruct((rows, n * cols), pieces[0].dtype),
        in_specs=[SMEM] + [ANY] * len(pieces),
        out_specs=ANY,
        scratch_shapes=[pltpu.SemaphoreType.DMA((n,))],
        name="join_columns",
    )(flat_index(t), *pieces)


def norm_kernel(n, count, t_ref, gain, bias, *refs):
    ins, out, stack, flat, sems = refs[:count], *refs[count:]
    t = t_ref[0]
    cols = ins[0].shape[-1]
    width = n * cols
    copies = [
        pltpu.make_async_copy(piece(ins, q), stack.at[device_of(t, q, n)], sems.at[q])
        for q in range(n)
    ]
    for copy in copies:
        copy.start()
    for copy in copies:
        copy.wait()
    total = 0.0
    for j in range(n):
        block = stack[j].astype(F32)
        flat[:, j * cols : (j + 1) * cols] = block
        total = total + jnp.sum(block, axis=1, keepdims=True)
    mean = total / width
    step = 1280
    spread = 0.0
    for k in range(0, width, step):
        centre = flat[:, k : k + step] - mean
        spread = spread + jnp.sum(centre * centre, axis=1, keepdims=True)
    scale = lax.rsqrt(spread / width + 1e-05)
    for k in range(0, width, step):
        centre = flat[:, k : k + step] - mean
        out[:, k : k + step] = (
            centre * scale * gain[:, k : k + step] + bias[:, k : k + step]
        ).astype(BF16)


def norm_features(pieces, gain, bias, t, n):
    rows, cols = pieces[0].shape[-2:]
    width = n * cols
    return pl.pallas_call(
        functools.partial(norm_kernel, n, len(pieces)),
        out_shape=jax.ShapeDtypeStruct((rows, width), BF16),
        in_specs=[SMEM, VMEM, VMEM] + [ANY] * len(pieces),
        out_specs=VMEM,
        scratch_shapes=[
            pltpu.VMEM((n, rows, cols), BF16),
            pltpu.VMEM((rows, width), F32),
            pltpu.SemaphoreType.DMA((n,)),
        ],
        name="norm_features",
    )(flat_index(t), gain[None], bias[None], *pieces)


GROUP = 8
DEPTH = 4


def lookup_kernel(count, ids, table, out, tiles, acc, sems):
    rows = out.shape[1]
    groups = count // GROUP
    acc[...] = jnp.zeros_like(acc)

    def copy(g, k):
        lane = pl.multiple_of(ids[g * GROUP + k] // 128 * 128, 128)
        slot = lax.rem(g, DEPTH)
        return pltpu.make_async_copy(
            table.at[:, pl.ds(lane, 128)],
            tiles.at[slot, :, pl.ds(k * 128, 128)],
            sems.at[slot, k],
        )

    def fetch(g):
        for k in range(GROUP):
            copy(g, k).start()

    for g in range(min(DEPTH - 1, groups)):
        fetch(g)
    sub = lax.broadcasted_iota(jnp.int32, (128, 128), 0)
    lane = lax.broadcasted_iota(jnp.int32, (128, 128), 1)

    def body(g, carry):
        @pl.when(g + DEPTH - 1 < groups)
        def _():
            fetch(g + DEPTH - 1)

        for k in range(GROUP):
            copy(g, k).wait()
        slot = lax.rem(g, DEPTH)
        first = lax.rem(g * GROUP, 128)
        picks = []
        for k in range(GROUP):
            column = lax.rem(ids[g * GROUP + k], 128)
            hit = (sub == column) & (lane == first + k)
            picks.append(jnp.where(hit, 1.0, 0.0).astype(BF16))
        pick = jnp.concatenate(picks, axis=0)
        acc[g * GROUP // 128] += jnp.dot(tiles[slot], pick, preferred_element_type=F32)
        return carry

    lax.fori_loop(0, groups, body, 0)
    for a in range(acc.shape[0]):
        upto = min(128, count - a * 128)
        out[a * 128 : a * 128 + upto, :] = acc[a].T[:upto].astype(BF16)


def lookup(table, ids):
    count, rows = ids.shape[0], table.shape[0]
    return pl.pallas_call(
        functools.partial(lookup_kernel, count),
        out_shape=jax.ShapeDtypeStruct((count, rows), BF16),
        in_specs=[SMEM, ANY],
        out_specs=VMEM,
        scratch_shapes=[
            pltpu.VMEM((DEPTH, rows, GROUP * 128), BF16),
            pltpu.VMEM((pl.cdiv(count, 128), rows, 128), F32),
            pltpu.SemaphoreType.DMA((DEPTH, GROUP)),
        ],
        name="lookup",
    )(ids, table)


PAD = 16


def decoder_kernel(n, count, t_ref, gain, hidden, gate, upw, *refs):
    ins = refs[:count]
    outs = refs[count : count + 4]
    inverse_out = refs[count + 4]
    tokens, normed, acc, dots, sems = refs[count + 5 :]
    step = pl.program_id(0)
    t = t_ref[0]
    rows, width = tokens.shape
    cols = width // n

    @pl.when(step == 0)
    def _():
        copies = []
        for q in range(n):
            at = pl.multiple_of(device_of(t, q, n) * cols, 128)
            copies.append(
                pltpu.make_async_copy(
                    piece(ins, q), tokens.at[:, pl.ds(at, cols)], sems.at[q]
                )
            )
        for copy in copies:
            copy.start()
        for copy in copies:
            copy.wait()
        square = 0.0
        span = 2 * cols
        for k in range(0, width, span):
            value = tokens[:, k : k + span].astype(F32)
            square = square + jnp.sum(value * value, axis=1, keepdims=True)
        inverse = lax.rsqrt(square / width + 1e-05)
        inverse_out[...] = jnp.broadcast_to(inverse, inverse_out.shape)
        for k in range(0, width, span):
            value = tokens[:, k : k + span].astype(F32)
            normed[:, k : k + span] = (value * inverse * gain[:, k : k + span]).astype(BF16)

    g = jnp.dot(normed[...], gate[...], preferred_element_type=F32)
    u = jnp.dot(normed[...], upw[...], preferred_element_type=F32)
    h = hidden[...]
    sig = jax.nn.sigmoid(g)
    gate_grad = (h * u * sig * (1.0 + g * (1.0 - sig))).astype(BF16)
    up_grad = (h * g * sig).astype(BF16)
    dot_part = jnp.sum(
        gate_grad.astype(F32) * g + up_grad.astype(F32) * u, axis=1, keepdims=True
    )
    last = (((1,), (1,)), ((), ()))
    span = 2 * cols
    for k in range(0, width, span):
        part = lax.dot_general(
            gate_grad, gate[k : k + span, :], last, preferred_element_type=F32
        ) + lax.dot_general(up_grad, upw[k : k + span, :], last, preferred_element_type=F32)

        @pl.when(step == 0)
        def _():
            acc[:, k : k + span] = part

        @pl.when(step > 0)
        def _():
            acc[:, k : k + span] += part

    @pl.when(step == 0)
    def _():
        dots[...] = jnp.broadcast_to(dot_part, dots.shape)

    @pl.when(step > 0)
    def _():
        dots[...] += jnp.broadcast_to(dot_part, dots.shape)

    @pl.when(step == pl.num_programs(0) - 1)
    def _():
        sub = lax.broadcasted_iota(jnp.int32, (rows, cols), 0)
        lane = lax.broadcasted_iota(jnp.int32, (rows, cols), 1)
        line = jnp.sum(
            jnp.where(sub == lane, jnp.broadcast_to(dots[:, :1], (rows, cols)), 0.0),
            axis=0,
            keepdims=True,
        )
        tail = jnp.broadcast_to(line, (PAD, cols)).astype(BF16)
        per = n // 4
        for q in range(n):
            at = pl.multiple_of(device_of(t, q, n) * cols, 128)
            outs[q // per][q % per, :rows, :] = acc[:, pl.ds(at, cols)].astype(BF16)
            outs[q // per][q % per, rows:, :] = tail


def decoder(pieces, gain, hidden, gate, upw, t, n):
    rows, cols = pieces[0].shape[-2:]
    width, units = gate.shape
    block = 256
    out = jax.ShapeDtypeStruct((n // 4, rows + PAD, cols), BF16)
    *parts, inverse = pl.pallas_call(
        functools.partial(decoder_kernel, n, len(pieces)),
        grid=(units // block,),
        out_shape=[out] * 4 + [jax.ShapeDtypeStruct((rows, 128), F32)],
        in_specs=[
            SMEM,
            VMEM,
            pl.BlockSpec((rows, block), lambda i: (0, i)),
            pl.BlockSpec((width, block), lambda i: (0, i)),
            pl.BlockSpec((width, block), lambda i: (0, i)),
        ]
        + [ANY] * len(pieces),
        out_specs=[VMEM] * 5,
        scratch_shapes=[
            pltpu.VMEM((rows, width), BF16),
            pltpu.VMEM((rows, width), BF16),
            pltpu.VMEM((rows, width), F32),
            pltpu.VMEM((rows, 128), F32),
            pltpu.SemaphoreType.DMA((n,)),
        ],
        compiler_params=pltpu.CompilerParams(
            dimension_semantics=("arbitrary",), vmem_limit_bytes=48 * 1024 * 1024
        ),
        name="decoder",
    )(flat_index(t), gain[None], hidden, gate, upw, *pieces)
    return parts, inverse[:, :1]


def live_slots(counts, per_image):
    ends = jnp.cumsum(counts)
    order = jnp.arange(LIVE, dtype=jnp.int32)
    past = (order[:, None] >= ends[None, :]).astype(jnp.int32)
    image = jnp.sum(past, axis=1)
    start = jnp.sum(past * counts[None, :], axis=1)
    return image * per_image + order - start


def one_hot(index, size):
    return index[:, None] == jnp.arange(size, dtype=jnp.int32)[None, :]


def pick(index, table):
    hit = one_hot(index, table.shape[0])
    return jnp.sum(jnp.where(hit, table[None, :], 0), axis=1)


def pick_rows(index, table):
    return jnp.dot(one_hot(index, table.shape[0]).astype(BF16), table)


def split_rows(
    n,
    image_features,
    image_counts,
    slot_position,
    text_ids,
    norm_gain,
    norm_bias,
    proj_first,
    proj_second,
    embedding,
    rms_gain,
    gate_weight,
    up_weight,
    down_weight,
    output_grad,
):
    slot_total = image_features.shape[0]
    seq_len, col_count = output_grad.shape
    width = gate_weight.shape[0]
    t = lax.axis_index(AX)

    slots = live_slots(image_counts, slot_total // image_counts.shape[0])
    features = pick_rows(slots, image_features)
    feature_blocks = gather_blocks(features, n)

    positions = pick(slots, slot_position)
    place = jnp.arange(seq_len, dtype=jnp.int32)
    hit = positions[:, None] == place[None, :]
    is_image = jnp.any(hit, axis=0)
    before = jnp.sum((positions[:, None] < place[None, :]).astype(jnp.int32), axis=0)
    image_at = jnp.sum(
        jnp.where(hit, jnp.arange(LIVE, dtype=jnp.int32)[:, None], 0), axis=0
    )
    row_of = jnp.where(is_image, image_at, LIVE + place - before)
    order = jnp.sum(
        jnp.where(row_of[:, None] == place[None, :], place[:, None], 0), axis=0
    )
    grad_rows = pick_rows(order, output_grad)
    grad_full = lax.all_gather(grad_rows, AX, axis=1, tiled=True)
    text_rows = lookup(embedding, pick(order[LIVE:], text_ids))
    text_stacks = gather_stacks(text_rows, n)

    normed = norm_features(feature_blocks, norm_gain, norm_bias, t, n)
    hidden_pre = lax.dot_general(
        normed, proj_first, (((1,), (1,)), ((), ())), preferred_element_type=F32
    )
    act_cols = jax.nn.gelu(hidden_pre, approximate=False).astype(BF16)
    act_full = join_columns(gather_blocks(act_cols, n), t, n)
    image_rows = lax.dot_general(
        act_full, proj_second, (((1,), (1,)), ((), ())), preferred_element_type=F32
    ).astype(BF16)
    image_blocks = gather_blocks(image_rows, n)

    hidden_grad = lax.dot_general(
        grad_full, down_weight, (((1,), (1,)), ((), ())), preferred_element_type=F32
    )
    gain_cols = lax.dynamic_slice_in_dim(rms_gain, t * col_count, col_count, 0)

    def finish(parts, inverse, rows, grads):
        count = rows.shape[0]
        total = scatter_sum(parts, n)
        norm_grad, row_dots = total[:count], total[count, :count]
        unit = rows.astype(F32) * inverse
        return grads.astype(F32) + inverse * (
            gain_cols * norm_grad - unit * (row_dots / width)[:, None]
        )

    text_parts, text_inverse = decoder(
        text_stacks, rms_gain, hidden_grad[LIVE:], gate_weight, up_weight, t, n
    )
    text_grad = finish(text_parts, text_inverse, text_rows, grad_rows[LIVE:])
    image_parts, image_inverse = decoder(
        image_blocks, rms_gain, hidden_grad[:LIVE], gate_weight, up_weight, t, n
    )
    image_grad = finish(image_parts, image_inverse, image_rows, grad_rows[:LIVE])
    second_grad = lax.dot_general(
        image_grad.astype(BF16), act_full, (((0,), (0,)), ((), ())), preferred_element_type=F32
    )
    input_grad = jnp.concatenate([image_grad, text_grad], axis=0)[row_of]
    return (input_grad, second_grad)


def all_rows(
    image_features,
    image_counts,
    slot_position,
    text_ids,
    norm_gain,
    norm_bias,
    proj_first,
    proj_second,
    embedding,
    rms_gain,
    gate_weight,
    up_weight,
    down_weight,
    output_grad,
):
    slot_total = image_features.shape[0]
    per_image = slot_total // image_counts.shape[0]
    seq_len = output_grad.shape[0]
    model_width = gate_weight.shape[0]
    col_count = output_grad.shape[1]
    packed_order = live_slots(image_counts, per_image)
    gathered = lax.all_gather(image_features[packed_order], AX, axis=1, tiled=True)
    positions = slot_position[packed_order]
    normed = layer_norm(gathered, norm_gain, norm_bias)
    hidden_pre = lax.dot_general(
        normed, proj_first, (((1,), (1,)), ((), ())), preferred_element_type=jnp.float32
    )
    act_cols = jax.nn.gelu(hidden_pre, approximate=False).astype(jnp.bfloat16)
    act_full = lax.all_gather(act_cols, AX, axis=1, tiled=True)
    projected = lax.dot_general(
        act_full, proj_second, (((1,), (1,)), ((), ())), preferred_element_type=jnp.float32
    ).astype(jnp.bfloat16)
    text_rows = jnp.take(embedding, text_ids, axis=1).T
    tokens = text_rows.at[positions].set(projected, mode="drop")
    full_tokens = lax.all_gather(tokens, AX, axis=1, tiled=True)
    values = full_tokens.astype(jnp.float32)
    inverse = lax.rsqrt(jnp.mean(values * values, axis=-1, keepdims=True) + 1e-05)
    normed_tokens = (values * inverse * rms_gain).astype(jnp.bfloat16)
    gate_out = jnp.dot(normed_tokens, gate_weight, preferred_element_type=jnp.float32)
    up_out = jnp.dot(normed_tokens, up_weight, preferred_element_type=jnp.float32)
    hidden_grad = lax.dot_general(
        lax.all_gather(output_grad, AX, axis=1, tiled=True),
        down_weight,
        (((1,), (1,)), ((), ())),
        preferred_element_type=jnp.float32,
    )
    sig_gate = jax.nn.sigmoid(gate_out)
    gate_grad = (hidden_grad * up_out * sig_gate * (1.0 + gate_out * (1.0 - sig_gate))).astype(
        jnp.bfloat16
    )
    up_grad = (hidden_grad * gate_out * sig_gate).astype(jnp.bfloat16)
    partial_value = lax.dot_general(
        gate_grad, gate_weight, (((1,), (1,)), ((), ())), preferred_element_type=jnp.float32
    )
    partial_value = partial_value + lax.dot_general(
        up_grad, up_weight, (((1,), (1,)), ((), ())), preferred_element_type=jnp.float32
    )
    norm_grad = lax.psum_scatter(partial_value, AX, scatter_dimension=1, tiled=True)
    offset = lax.axis_index(AX) * col_count
    gain_cols = lax.dynamic_slice_in_dim(rms_gain, offset, col_count, 0)
    unit_cols = tokens.astype(jnp.float32) * inverse
    scaled = gain_cols * norm_grad
    row_sums = lax.psum(jnp.sum(scaled * unit_cols, axis=-1), AX)
    input_grad = output_grad.astype(jnp.float32) + inverse * (
        scaled - unit_cols * (row_sums / model_width)[:, None]
    )
    proj_grad = input_grad[positions].astype(jnp.bfloat16)
    second_grad = lax.dot_general(
        proj_grad, act_full, (((0,), (0,)), ((), ())), preferred_element_type=jnp.float32
    )
    return (input_grad, second_grad)


def solution(mesh):
    n = mesh.shape[AX]

    def on_device(*args):
        col_count, units = args[13].shape[1], args[10].shape[1]
        aligned = n % 4 == 0 and col_count % 128 == 0 and units % 256 == 0
        return split_rows(n, *args) if aligned else all_rows(*args)

    placed = (
        P("groups", "tensor"),
        P("groups"),
        P("groups"),
        P("groups"),
        P(),
        P(),
        P("tensor", None),
        P("tensor", None),
        P("tensor", None),
        P(),
        P(None, "tensor"),
        P(None, "tensor"),
        P("tensor", None),
        P("groups", "tensor"),
    )
    return jax.shard_map(
        on_device,
        mesh=mesh,
        in_specs=placed,
        out_specs=(P("groups", "tensor"), P(("groups", "tensor"), None)),
        check_vma=False,
    )
```
